512 devices in a mesh: tp: 8 (over x, core), ep: 64 (over z, y).
Axes of the slice: x: 4, y: 4, z: 16, core: 2. Of those that a mesh axis runs over, the one named last changes fastest.
Arguments:
- hidden_in: bfloat16 [4096, 4096], P(('ep', 'tp')), may hold values from -6 to 6
- norm_gain: bfloat16 [4096], replicated, may hold values from 0.099609375 to 1.8984375
- expert_ids: int32 [4096, 8], P('ep'), may hold values from 0 to 63, all different within a row; in each aligned block of 64 rows (0 to 63, 64 to 127, ...) at most 16 rows name the same one
- gate_weights: float32 [4096, 8], P('ep'), may hold values from 0.05 to 0.35
- w_gate: bfloat16 [64, 4096, 1024], P('ep', None, 'tp'), may hold values from -0.09375 to 0.09375
- w_up: bfloat16 [64, 4096, 1024], P('ep', None, 'tp'), may hold values from -0.09375 to 0.09375
- w_down: bfloat16 [64, 1024, 4096], P('ep', None, 'tp'), may hold values from -0.1875 to 0.1875
Outputs:
- mixed: bfloat16 [4096, 4096], P('ep', 'tp')
The draws below stay inside these ranges and needn't reach their ends.
Inputs may be any that keep to these rules, and one draw needn't show every extreme that they name: `expert_ids`: each row names 8 different experts. Tokens form groups of 64 consecutive rows; within one group no expert is named by more than 16 rows, and in every draw some expert is named by exactly 16 rows of some group.
All inputs are finite; a program needn't handle non-finite values.
Results may differ from the reference program's by a relative error of at most 0.0043.
Values may be sent and summed in bfloat16 or wider, within the bound.
A program may use at most 64 MiB of HBM per device.

```python
import math
import jax
import jax.numpy as jnp
import numpy as np
from jax import lax

D = 4096
HID = 1024
EXPERTS = 64
TOP = 8
GROUP = 64
CAP = 16
TOKENS = 4096
N_EP = 64


def level_of(rng, dims, shards, smallest, high):
    def one(axis_at, blocks):
        heights = jax.random.uniform(jax.random.fold_in(jax.random.fold_in(rng, 6), axis_at), (blocks,), jnp.float32, smallest / len(shards), high / len(shards))
        return jnp.repeat(jnp.exp(heights), dims[axis_at] // blocks).reshape((-1,) + (1,) * (len(dims) - axis_at - 1))

    loudness = one(*shards[0])
    for cut in shards[1:]:
        loudness = loudness * one(*cut)
    return loudness


def shared_out(own_key, own, number, rows, number_of, top, bound, slope):
    sequence = jax.random.permutation(own_key, number_of)
    crowded, ordinary = portions_of(number_of, rows * top, bound, slope, True), portions_of(number_of, rows * top, bound, slope, False)
    places = jnp.arange(number_of)

    def named(lengths, offset_by):
        used = int((lengths > 0).sum())
        fixed = max(1, used // 4)
        moved = fixed + (places - fixed + offset_by * (used - fixed)) % max(1, number_of - fixed)
        return jnp.zeros((number_of,), jnp.int32).at[sequence[jnp.where(places < fixed, places, moved)]].set(jnp.asarray(lengths, jnp.int32))

    lengths = jnp.where(number % 4 == 0, named(crowded, number // 4), named(ordinary, number - number // 4 - 1))
    mixed = jax.random.permutation(jax.random.fold_in(own, 3), number_of)
    source_of, sink = mixed[0:number_of // 2 * 2:2], mixed[1:number_of // 2 * 2:2]
    slack = jnp.minimum(lengths[source_of] - 1, bound - lengths[sink]) // 2
    slack = jnp.where((source_of == sequence[0]) | (sink == sequence[0]) | (lengths[sink] == 0), 0, jnp.maximum(slack, 0))
    moved = jax.random.randint(jax.random.fold_in(own, 4), (number_of // 2,), 0, 1 << 20) % (slack + 1)
    lengths = lengths.at[source_of].add(-moved).at[sink].add(moved)
    labels = jnp.searchsorted(jnp.cumsum(lengths), jnp.arange(rows * top), side="right").astype(jnp.int32)
    table = labels.reshape(top, rows).T
    table = table[jax.random.permutation(jax.random.fold_in(own, 1), rows)]
    offset_by = jax.random.randint(jax.random.fold_in(own, 2), (rows, 1), 0, top)
    return jnp.take_along_axis(table, (jnp.arange(top)[None, :] + offset_by) % top, axis=1)


def portions_of(number_of, total, bound, slope, full):
    loads = [(1 << 20) // math.isqrt(grade ** slope) + 1 for grade in range(1, number_of + 1)]
    largest = bound if full else min(bound, max(-(-total // number_of), total * loads[0] // sum(loads)))
    least = 1 if total - largest >= number_of - 1 else 0
    counts, rest = [largest] + [least] * (number_of - 1), total - largest - least * (number_of - 1)
    while rest > 0:
        free = [i for i in range(1, number_of) if counts[i] < largest] or [i for i in range(1, number_of) if counts[i] < bound]
        mass, remaining = sum([loads[i] for i in free]), rest
        for i in free:
            extra = min(bound - counts[i], max(1, remaining * loads[i] // mass), rest)
            counts[i] = counts[i] + extra
            rest = rest - extra
    return np.array(counts)


def scatter_about(rng, shape, spread, most, cuts=(), kind=jnp.bfloat16):
    gain = level_of(rng, shape, cuts, -0.22, 0.18) if cuts else 1.0
    result = jax.random.normal(rng, shape, jnp.float32) * spread * gain
    return jnp.minimum(jnp.maximum(result, -most), most).astype(kind)


def setup_inputs(seed: int = 0) -> dict:
    streams_of = jax.random.split(jax.random.key(seed), 8)
    hidden_in = scatter_about(streams_of[0], (TOKENS, D), 1.0, 6.0, ((0, 512),))
    norm_gain = jnp.clip(1.0 + 0.18 * jax.random.normal(streams_of[1], (D,), jnp.float32), 0.099609375, 1.8984375).astype(jnp.bfloat16)
    expert_ids_keys = jax.random.split(jax.random.fold_in(streams_of[2], 1), TOKENS // GROUP)
    expert_ids_turns = jax.random.permutation(jax.random.fold_in(streams_of[2], 3), TOKENS // GROUP)
    expert_ids = jax.vmap(lambda own, number: shared_out(jax.random.fold_in(streams_of[2], 2), own, number, GROUP, EXPERTS, TOP, CAP, 2))(expert_ids_keys, expert_ids_turns).reshape((TOKENS, TOP))
    gate_weights = jnp.clip(0.05 + 0.29999999 * jax.random.uniform(streams_of[3], (TOKENS, TOP), jnp.float32) ** level_of(streams_of[3], (TOKENS, TOP), ((0, 64),), -0.2, 0.2), 0.05, 0.35)
    w_gate = scatter_about(streams_of[4], (EXPERTS, D, HID), D ** -0.5, 0.09375, ((0, 64), (2, 8)))
    w_up = scatter_about(streams_of[5], (EXPERTS, D, HID), D ** -0.5, 0.09375, ((0, 64), (2, 8)))
    w_down = scatter_about(streams_of[6], (EXPERTS, HID, D), HID ** -0.5, 0.1875, ((0, 64), (2, 8)))
    return dict(hidden_in=hidden_in, norm_gain=norm_gain, expert_ids=expert_ids, gate_weights=gate_weights, w_gate=w_gate, w_up=w_up, w_down=w_down)


def reference(hidden_in, norm_gain, expert_ids, gate_weights, w_gate, w_up, w_down):
    values = hidden_in.astype(jnp.float32)
    scale = lax.rsqrt(lax.optimization_barrier(jnp.mean(values * values, axis=1, keepdims=True)) + 1e-06)
    normed = (values * scale * norm_gain.astype(jnp.float32)).astype(jnp.bfloat16)
    flat_ids = expert_ids.reshape(-1)
    flat_gates = gate_weights.reshape(-1)
    window = N_EP * CAP

    def one_expert(total, expert):
        live = flat_ids == expert
        picks = jnp.nonzero(live, size=window, fill_value=0)[0].astype(jnp.int32)
        valid = jnp.arange(window, dtype=jnp.int32) < jnp.sum(live.astype(jnp.int32))
        weights = jnp.where(valid, flat_gates[picks], jnp.zeros((), flat_gates.dtype))
        token_rows = (picks // TOP).astype(jnp.int32)
        rows = normed[token_rows]
        gate_act = jnp.dot(rows, w_gate[expert], preferred_element_type=jnp.float32)
        up_act = jnp.dot(rows, w_up[expert], preferred_element_type=jnp.float32)
        hidden = (jax.nn.silu(gate_act) * up_act).astype(jnp.bfloat16)
        expert_out = jnp.dot(hidden, w_down[expert], preferred_element_type=jnp.float32).astype(jnp.bfloat16)
        term = weights[:, None] * expert_out.astype(total.dtype)
        return (total.at[token_rows].add(term), None)
    start = jnp.zeros((TOKENS, D), jnp.float32)
    total, _ = lax.scan(one_expert, start, jnp.arange(EXPERTS, dtype=jnp.int32))
    return (values + total).astype(jnp.bfloat16)
```

```python
import functools

import jax
import jax.numpy as jnp
from jax import lax
from jax.experimental import pallas as pl
from jax.experimental.pallas import tpu as pltpu
from jax.sharding import PartitionSpec as P

MESH = pl.DeviceIdType.MESH
F32, BF16 = jnp.float32, jnp.bfloat16
STEPS = 8
AT = dict(Y=1, X1=3, X2=5, M=6, H2=8, D=9, C=11)


def kernel(
    hid_ref, gain_ref, ids_ref, gat_ref, wg_ref, wu_ref, wd_ref, out_ref,
    hq, scl, ring_a, ring_b, meta_a, meta_b, pick, ybuf, xfull, hfull, obuf, oin, cbuf, own, zin_a, zin_b,
    wcat, wdv, tri,
    wsem, p_s, p_r, za_s, za_r, zb_s, zb_r, y_s, y_r, x_s, x_r, h_s, h_r, o_s, o_r, ra_s, ra_r, rb_s, rb_r,
):
    tp, ep = lax.axis_index("tp"), lax.axis_index("ep")
    x, c = tp // 2, lax.rem(tp, 2)
    z, y = ep // 4, lax.rem(ep, 4)
    quarter = lax.rem(tp, 4)
    across = lax.rem(quarter + 2, 4)

    def at_tp(r):
        return (lax.rem(tp + r + 8, 8), ep)

    def at_x(r):
        return (lax.rem(x + r + 4, 4) * 2 + c, ep)

    def at_y(r):
        return (tp, z * 4 + lax.rem(y + r, 4))

    def at_z(r):
        return (tp, lax.rem(z + r + 16, 16) * 4 + y)

    partner = (x * 2 + 1 - c, ep)

    def move(src, dst, send, recv, device):
        return pltpu.make_async_remote_copy(
            src_ref=src, dst_ref=dst, send_sem=send, recv_sem=recv, device_id=device, device_id_type=MESH
        )

    barrier = pltpu.get_barrier_semaphore()
    peers = [at_tp(r) for r in range(1, 8)] + [at_y(r) for r in range(1, 4)]
    peers += [at_z(r) for r in (-4, -3, -2, -1, 1, 2, 3, 4)]
    for peer in peers:
        pl.semaphore_signal(barrier, inc=1, device_id=peer, device_id_type=MESH)

    loads = []
    for q in range(4):
        for b in range(2):
            rows = pl.ds((q + 4 * b) * 512, 512)
            for n, w in enumerate((wg_ref, wu_ref)):
                loads.append(
                    pltpu.make_async_copy(
                        w.at[0, rows, :], wcat.at[q, pl.ds(b * 512, 512), pl.ds(n * 128, 128)], wsem.at[len(loads)]
                    )
                )
    loads.append(pltpu.make_async_copy(wd_ref.at[0], wdv, wsem.at[16]))
    for load in loads:
        load.start()

    values = hid_ref[...].astype(F32)
    scale = lax.rsqrt(jnp.mean(values * values, axis=1, keepdims=True) + 1e-06)
    scl[tp] = jnp.broadcast_to(scale, (8, 128))
    for b in range(2):
        hq[tp, b] = hid_ref[:, pl.ds(pl.multiple_of((quarter + 4 * b) * 512, 512), 512)]
    ids, gates = ids_ref[...].astype(F32), gat_ref[...]
    meta = jnp.concatenate(
        [jnp.concatenate([ids, ids], axis=1), jnp.concatenate([gates, gates], axis=1)], axis=0
    )
    meta_a[0] = meta
    meta_b[0] = meta
    before, after = lax.broadcasted_iota(jnp.int32, (128, 128), 0), lax.broadcasted_iota(jnp.int32, (128, 128), 1)
    tri[...] = ((before < after) & ((before < 64) == (after < 64))).astype(F32).astype(BF16)
    pl.semaphore_wait(barrier, len(peers))

    def spread(r, b):
        device = at_tp(r)
        if b == 2:
            src, dst = scl.at[tp], scl.at[tp]
        else:
            block = lax.rem(device[0], 4) + 4 * b
            src, dst = hid_ref.at[:, pl.ds(pl.multiple_of(block * 512, 512), 512)], hq.at[tp, b]
        return move(src, dst, p_s.at[r - 1, b], p_r.at[r - 1, b], device)

    for r in range(1, 8):
        for b in range(3):
            spread(r, b).start()
    for r in range(1, 8):
        for b in range(3):
            spread(r, b).wait_recv()
    scales = scl[...]
    scales = jnp.concatenate([scales] * 4, axis=2)
    for b in range(2):
        gain = gain_ref[pl.ds(quarter + 4 * b, 1), :]
        normed = (hq[:, b].astype(F32) * scales).reshape(64, 512) * gain
        normed = normed.astype(BF16)
        ring_a[0, b] = normed
        ring_b[0, b] = normed
    for load in loads:
        load.wait()

    def up(i, b):
        if b == 2:
            src, dst = meta_a.at[i], meta_a.at[i + 1]
        else:
            src, dst = ring_a.at[i, b], ring_a.at[i + 1, b]
        return move(src, dst, za_s.at[i, b], za_r.at[i, b], at_z(1))

    def down(i, b):
        if b == 2:
            src, dst = meta_b.at[i], meta_b.at[i + 1]
        else:
            src, dst = ring_b.at[i, b], ring_b.at[i + 1, b]
        return move(src, dst, zb_s.at[i, b], zb_r.at[i, b], at_z(-1))

    def to_y(j, r):
        device = at_y(r)
        there = lax.rem(y + r, 4)
        dst = xfull.at[j, quarter, pl.ds(pl.multiple_of(y * 32, 32), 32), :]
        return move(ybuf.at[j, there], dst, y_s.at[j, r - 1], y_r.at[j, r - 1], device)

    def to_x(j, n):
        if n == 0:
            part, device = xfull.at[j, quarter, pl.ds(0, 64), :], at_x(1)
        elif n == 1:
            part, device = xfull.at[j, quarter, pl.ds(64, 64), :], at_x(-1)
        elif n == 2:
            part, device = xfull.at[j, quarter], partner
        else:
            part, device = xfull.at[j, across], partner
        return move(part, part, x_s.at[j, n], x_r.at[j, n], device)

    def to_h(j, n):
        if n < 3:
            part, device = hfull.at[j, tp], at_x(n + 1)
        elif n == 3:
            part, device = hfull.at[j, tp], partner
        else:
            part, device = hfull.at[j, lax.rem(tp - 2 * (n - 3) + 8, 8)], partner
        return move(part, part, h_s.at[j, n], h_r.at[j, n], device)

    def to_o(j, r):
        return move(obuf.at[j, lax.rem(y + r, 4)], oin.at[j, y], o_s.at[j, r - 1], o_r.at[j, r - 1], at_y(r))

    def home_a(j, hops):
        return move(cbuf.at[j, 0], zin_a.at[j], ra_s.at[j], ra_r.at[j], at_z(-hops))

    def home_b(j, hops):
        return move(cbuf.at[j, 1], zin_b.at[j], rb_s.at[j], rb_r.at[j], at_z(hops))

    def stage_y(j):
        first = lax.broadcasted_iota(jnp.int32, (8, 128), 1) < 64
        ids = jnp.where(first, meta_a[j + 1, 0:8, :], meta_b[j, 0:8, :])
        gates = jnp.where(first, meta_a[j + 1, 8:16, :], meta_b[j, 8:16, :])
        row = lax.broadcasted_iota(jnp.int32, (16, 128), 0)
        hits, weights, table = [], [], jnp.zeros((16, 128), F32)
        for n in range(4):
            same = ids == (z * 4 + n).astype(F32)
            hits.append(jnp.sum(jnp.where(same, 1.0, 0.0), axis=0, keepdims=True))
            weights.append(jnp.sum(jnp.where(same, gates, 0.0), axis=0, keepdims=True))
            table = jnp.where(row == n, hits[n], table)
        places = jnp.dot(table.astype(BF16), tri[...], preferred_element_type=F32)
        slot = lax.broadcasted_iota(jnp.int32, (32, 128), 0).astype(F32)
        shift = jnp.where(first[0:1], 0.0, 16.0)
        chosen, weighted = [], []
        for n in range(4):
            mine = jnp.where(hits[n] > 0.5, places[n : n + 1] + shift, -1.0)
            chosen.append(jnp.where(slot == mine, 1.0, 0.0))
            weighted.append(chosen[n] * weights[n])
        chosen = jnp.concatenate(chosen, axis=0).astype(BF16)
        weighted = jnp.concatenate(weighted, axis=0)
        high = weighted.astype(BF16)
        pick[j, 0] = high
        pick[j, 1] = (weighted - high.astype(F32)).astype(BF16)
        for b in range(2):
            tokens = jnp.concatenate([ring_a[j + 1, b], ring_b[j, b]], axis=0)
            rows = jnp.dot(chosen, tokens, preferred_element_type=F32).astype(BF16)
            ybuf[j, :, :, pl.ds(b * 512, 512)] = rows.reshape(4, 32, 512)
        xfull[j, quarter, pl.ds(pl.multiple_of(y * 32, 32), 32), :] = ybuf[j, y]
        for r in range(1, 4):
            to_y(j, r).start()

    def stage_x1(j):
        for r in range(1, 4):
            to_y(j, r).wait_recv()
        for n in range(3):
            to_x(j, n).start()

    def stage_x2(j):
        for n in range(2):
            wait_x(j, n)
        to_x(j, 3).start()

    def wait_x(j, n):
        part = xfull.at[j, across, pl.ds(64 * n, 64), :]
        move(part, part, x_s.at[j, n], x_r.at[j, n], partner).wait_recv()

    def stage_m(j):
        for n in range(2, 4):
            to_x(j, n).wait_recv()
        total = jnp.zeros((128, 256), F32)
        for q in range(4):
            total += jnp.dot(xfull[j, q], wcat[q], preferred_element_type=F32)
        gate, lift = total[:, :128], total[:, 128:]
        hfull[j, tp] = (gate / (1.0 + jnp.exp(-gate)) * lift).astype(BF16)
        for n in range(4):
            to_h(j, n).start()

    def stage_h2(j):
        for n in range(3):
            to_h(j, n).wait_recv()
        for n in range(4, 7):
            to_h(j, n).start()

    def stage_d(j):
        for n in range(3, 7):
            to_h(j, n).wait_recv()
        units = jnp.concatenate([hfull[j, n] for n in range(8)], axis=1)
        rows = jnp.dot(units, wdv[...], preferred_element_type=F32).astype(BF16)
        obuf[j] = rows.reshape(4, 32, 512)
        oin[j, y] = obuf[j, y]
        for r in range(1, 4):
            to_o(j, r).start()

    def stage_c(j):
        for r in range(1, 4):
            to_o(j, r).wait_recv()
        rows = oin[j].reshape(128, 512)
        dims = (((0,), (0,)), ((), ()))
        total = lax.dot_general(pick[j, 0], rows, dims, preferred_element_type=F32)
        total += lax.dot_general(pick[j, 1], rows, dims, preferred_element_type=F32)
        cbuf[j, 0] = total[:64].astype(BF16)
        cbuf[j, 1] = total[64:].astype(BF16)

        @pl.when(j < 3)
        def _():
            home_a(j, j + 1).start()

        @pl.when(j == 3)
        def _():
            own[0] = total[:64]

        @pl.when(j > 3)
        def _():
            home_a(j, j - 3).start()

        @pl.when(j == 0)
        def _():
            own[1] = total[64:]

        @pl.when((j > 0) & (j < 4))
        def _():
            home_b(j, j).start()

        @pl.when(j == 4)
        def _():
            own[2] = total[64:]

        @pl.when(j > 4)
        def _():
            home_b(j, j - 4).start()

    def stage(name, body, i):
        j = i - AT[name]

        @pl.when((j >= 0) & (j < STEPS))
        def _():
            body(j)

    @pl.loop(0, STEPS + AT["C"])
    def _(i):
        @pl.when(i <= STEPS)
        def _():
            for b in (2, 0, 1):

                @pl.when(i > 0)
                def _():
                    up(i - 1, b).wait_recv()

                @pl.when(i < STEPS)
                def _():
                    up(i, b).start()

                @pl.when((i > 0) & (i < STEPS))
                def _():
                    down(i - 1, b).wait_recv()

                @pl.when(i < STEPS - 1)
                def _():
                    down(i, b).start()

        stage("Y", stage_y, i)
        stage("X1", stage_x1, i)
        stage("X2", stage_x2, i)
        stage("H2", stage_h2, i)
        stage("D", stage_d, i)
        stage("M", stage_m, i)
        stage("C", stage_c, i)

    total = own[0]
    for j in range(4, 8):
        home_a(j, 0).wait_recv()
        total += zin_a[j].astype(F32)
    cbuf[3, 0] = total.astype(BF16)
    home_a(3, 4).start()
    total = own[2]
    for j in range(5, 8):
        home_b(j, 0).wait_recv()
        total += zin_b[j].astype(F32)
    cbuf[4, 1] = total.astype(BF16)
    home_b(4, 4).start()

    total = own[1] + hq[:, tp // 4].astype(F32).reshape(64, 512)
    for j in range(3):
        home_a(j, 0).wait_recv()
        total += zin_a[j].astype(F32)
    for j in range(1, 4):
        home_b(j, 0).wait_recv()
        total += zin_b[j].astype(F32)
    home_a(3, 4).wait_recv()
    home_b(4, 4).wait_recv()
    out_ref[...] = (total + zin_a[3].astype(F32) + zin_b[4].astype(F32)).astype(BF16)

    for r in range(1, 8):
        for b in range(3):
            spread(r, b).wait_send()

    @pl.loop(0, STEPS)
    def _(j):
        for b in range(3):
            up(j, b).wait_send()

            @pl.when(j < STEPS - 1)
            def _():
                down(j, b).wait_send()

        for r in range(1, 4):
            to_y(j, r).wait_send()
            to_o(j, r).wait_send()
        for n in range(4):
            to_x(j, n).wait_send()
        for n in range(7):
            to_h(j, n).wait_send()
        home_a(j, 1).wait_send()

        @pl.when(j > 0)
        def _():
            home_b(j, 1).wait_send()


def shards(hidden_in, norm_gain, expert_ids, gate_weights, w_gate, w_up, w_down):
    vmem, hbm = pl.BlockSpec(memory_space=pltpu.VMEM), pl.BlockSpec(memory_space=pl.ANY)
    dma = pltpu.SemaphoreType.DMA
    return pl.pallas_call(
        kernel,
        out_shape=jax.ShapeDtypeStruct((64, 512), BF16),
        in_specs=[vmem] * 4 + [hbm] * 3,
        out_specs=vmem,
        scratch_shapes=[
            pltpu.VMEM((8, 2, 8, 512), BF16),
            pltpu.VMEM((8, 8, 128), F32),
            pltpu.VMEM((9, 2, 64, 512), BF16),
            pltpu.VMEM((8, 2, 64, 512), BF16),
            pltpu.VMEM((9, 16, 128), F32),
            pltpu.VMEM((8, 16, 128), F32),
            pltpu.VMEM((8, 2, 128, 128), BF16),
            pltpu.VMEM((8, 4, 32, 1024), BF16),
            pltpu.VMEM((8, 4, 128, 1024), BF16),
            pltpu.VMEM((8, 8, 128, 128), BF16),
            pltpu.VMEM((8, 4, 32, 512), BF16),
            pltpu.VMEM((8, 4, 32, 512), BF16),
            pltpu.VMEM((8, 2, 64, 512), BF16),
            pltpu.VMEM((3, 64, 512), F32),
            pltpu.VMEM((8, 64, 512), BF16),
            pltpu.VMEM((8, 64, 512), BF16),
            pltpu.VMEM((4, 1024, 256), BF16),
            pltpu.VMEM((1024, 512), BF16),
            pltpu.VMEM((128, 128), BF16),
            dma((17,)),
            dma((7, 3)), dma((7, 3)),
            dma((8, 3)), dma((8, 3)),
            dma((7, 3)), dma((7, 3)),
            dma((8, 3)), dma((8, 3)),
            dma((8, 4)), dma((8, 4)),
            dma((8, 7)), dma((8, 7)),
            dma((8, 3)), dma((8, 3)),
            dma((8,)), dma((8,)),
            dma((8,)), dma((8,)),
        ],
        compiler_params=pltpu.CompilerParams(
            collective_id=0, has_side_effects=True, vmem_limit_bytes=56 * 1024 * 1024
        ),
    )(
        hidden_in,
        norm_gain.astype(F32).reshape(8, 512),
        expert_ids.T,
        gate_weights.T,
        w_gate,
        w_up,
        w_down,
    )


def solution(mesh):
    in_specs = (
        P(("ep", "tp"), None),
        P(),
        P("ep", None),
        P("ep", None),
        P("ep", None, "tp"),
        P("ep", None, "tp"),
        P("ep", None, "tp"),
    )
    return jax.shard_map(shards, mesh=mesh, in_specs=in_specs, out_specs=P("ep", "tp"), check_vma=False)
```

```python
import functools

import jax
import jax.numpy as jnp
from jax import lax
from jax.experimental import pallas as pl
from jax.experimental.pallas import tpu as pltpu
from jax.sharding import PartitionSpec as P

MESH = pl.DeviceIdType.MESH
F32, BF16 = jnp.float32, jnp.bfloat16
STEPS = 8
PARTS = 4
NEXT = {8: 6, 7: 6, 6: 3, 5: 3, 4: 3, 3: 0, 2: 0, 1: 0}
HOLDS = sorted({d for d in NEXT.values() if d}, reverse=True)
AT = dict(Y=1, X1=2, X2=4, M=5, H2=7, D=8, C=10)


def kernel(
    hid_ref, gain_ref, ids_ref, gat_ref, wg_ref, wu_ref, wd_ref, out_ref,
    hq, scl, ring_a, ring_b, meta_a, meta_b, pick, ybuf, xfull, hfull, obuf, oin, cbuf, own, zin_a, zin_b,
    wcat, wdv, tri,
    wsem, p_s, p_r, za_s, za_r, zb_s, zb_r, y_s, y_r, x_s, x_r, h_s, h_r, o_s, o_r, ra_s, ra_r, rb_s, rb_r,
):
    tp, ep = lax.axis_index("tp"), lax.axis_index("ep")
    x, c = tp // 2, lax.rem(tp, 2)
    z, y = ep // 4, lax.rem(ep, 4)
    quarter = lax.rem(tp, 4)
    across = lax.rem(quarter + 2, 4)

    def at_tp(r):
        return (lax.rem(tp + r + 8, 8), ep)

    def at_x(r):
        return (lax.rem(x + r + 4, 4) * 2 + c, ep)

    def at_y(r):
        return (tp, z * 4 + lax.rem(y + r, 4))

    def at_z(r):
        return (tp, lax.rem(z + r + 16, 16) * 4 + y)

    partner = (x * 2 + 1 - c, ep)

    def move(src, dst, send, recv, device):
        return pltpu.make_async_remote_copy(
            src_ref=src, dst_ref=dst, send_sem=send, recv_sem=recv, device_id=device, device_id_type=MESH
        )

    barrier = pltpu.get_barrier_semaphore()
    peers = [at_tp(r) for r in range(1, 8)] + [at_y(r) for r in range(1, 4)]
    hops = sorted({d - e for d, e in NEXT.items()} | {1})
    peers += [at_z(r) for h in hops for r in (h, -h)]
    for peer in peers:
        pl.semaphore_signal(barrier, inc=1, device_id=peer, device_id_type=MESH)

    values = hid_ref[...].astype(F32)
    scale = lax.rsqrt(jnp.mean(values * values, axis=1, keepdims=True) + 1e-06)
    scl[tp] = jnp.broadcast_to(scale, (8, 128))
    for b in range(2):
        hq[tp, b] = hid_ref[:, pl.ds(pl.multiple_of((quarter + 4 * b) * 512, 512), 512)]
    pl.semaphore_wait(barrier, len(peers))

    def spread(r, b):
        device = at_tp(r)
        if b == 2:
            src, dst = scl.at[tp], scl.at[tp]
        else:
            block = lax.rem(device[0], 4) + 4 * b
            src, dst = hid_ref.at[:, pl.ds(pl.multiple_of(block * 512, 512), 512)], hq.at[tp, b]
        return move(src, dst, p_s.at[r - 1, b], p_r.at[r - 1, b], device)

    for r in range(1, 8):
        for b in range(3):
            spread(r, b).start()
    loads = []
    for q in range(4):
        for b in range(2):
            rows = pl.ds((q + 4 * b) * 512, 512)
            for n, w in enumerate((wg_ref, wu_ref)):
                loads.append(
                    pltpu.make_async_copy(
                        w.at[0, rows, :], wcat.at[q, pl.ds(b * 512, 512), pl.ds(n * 128, 128)], wsem.at[len(loads)]
                    )
                )
    loads.append(pltpu.make_async_copy(wd_ref.at[0], wdv, wsem.at[16]))
    for load in loads:
        load.start()
    ids, gates = ids_ref[...].astype(F32), gat_ref[...]
    meta = jnp.concatenate(
        [jnp.concatenate([ids, ids], axis=1), jnp.concatenate([gates, gates], axis=1)], axis=0
    )
    meta_a[0] = meta
    meta_b[0] = meta
    before, after = lax.broadcasted_iota(jnp.int32, (128, 128), 0), lax.broadcasted_iota(jnp.int32, (128, 128), 1)
    tri[...] = ((before < after) & ((before < 64) == (after < 64))).astype(F32).astype(BF16)
    for r in range(1, 8):
        for b in range(3):
            spread(r, b).wait_recv()
    scales = scl[...]
    scales = jnp.concatenate([scales] * 4, axis=2)
    for b in range(2):
        gain = gain_ref[pl.ds(pl.multiple_of((quarter + 4 * b) * 512, 512), 512)].astype(F32).reshape(1, 512)
        normed = (hq[:, b].astype(F32) * scales).reshape(64, 512) * gain
        normed = normed.astype(BF16)
        ring_a[0, b] = normed
        ring_b[0, b] = normed
    for load in loads:
        load.wait()

    def up(i, b):
        if b == PARTS:
            src, dst = meta_a.at[i], meta_a.at[i + 1]
        else:
            cols = pl.ds(b * 1024 // PARTS % 512, 1024 // PARTS)
            src, dst = ring_a.at[i, b * 2 // PARTS, :, cols], ring_a.at[i + 1, b * 2 // PARTS, :, cols]
        return move(src, dst, za_s.at[i, b], za_r.at[i, b], at_z(1))

    def down(i, b):
        if b == PARTS:
            src, dst = meta_b.at[i], meta_b.at[i + 1]
        else:
            cols = pl.ds(b * 1024 // PARTS % 512, 1024 // PARTS)
            src, dst = ring_b.at[i, b * 2 // PARTS, :, cols], ring_b.at[i + 1, b * 2 // PARTS, :, cols]
        return move(src, dst, zb_s.at[i, b], zb_r.at[i, b], at_z(-1))

    def to_y(j, r):
        device = at_y(r)
        there = lax.rem(y + r, 4)
        dst = xfull.at[j, quarter, pl.ds(pl.multiple_of(y * 32, 32), 32), :]
        return move(ybuf.at[j, there], dst, y_s.at[j, r - 1], y_r.at[j, r - 1], device)

    def to_x(j, n):
        if n == 0:
            part, device = xfull.at[j, quarter, pl.ds(0, 64), :], at_x(1)
        elif n == 1:
            part, device = xfull.at[j, quarter, pl.ds(64, 64), :], at_x(-1)
        elif n == 2:
            part, device = xfull.at[j, quarter], partner
        else:
            part, device = xfull.at[j, across], partner
        return move(part, part, x_s.at[j, n], x_r.at[j, n], device)

    def to_h(j, n):
        if n < 3:
            part, device = hfull.at[j, tp], at_x(n + 1)
        elif n == 3:
            part, device = hfull.at[j, tp], partner
        else:
            part, device = hfull.at[j, lax.rem(tp - 2 * (n - 3) + 8, 8)], partner
        return move(part, part, h_s.at[j, n], h_r.at[j, n], device)

    def to_o(j, r):
        return move(obuf.at[j, lax.rem(y + r, 4)], oin.at[j, y], o_s.at[j, r - 1], o_r.at[j, r - 1], at_y(r))

    def home_a(j, d):
        return move(cbuf.at[j, 0], zin_a.at[j], ra_s.at[j], ra_r.at[j], at_z(NEXT[d] - d))

    def home_b(j, d):
        return move(cbuf.at[j, 1], zin_b.at[j], rb_s.at[j], rb_r.at[j], at_z(d - NEXT[d]))

    def stage_y(j):
        first = lax.broadcasted_iota(jnp.int32, (8, 128), 1) < 64
        ids = jnp.where(first, meta_a[j + 1, 0:8, :], meta_b[j, 0:8, :])
        gates = jnp.where(first, meta_a[j + 1, 8:16, :], meta_b[j, 8:16, :])
        row = lax.broadcasted_iota(jnp.int32, (16, 128), 0)
        hits, weights, table = [], [], jnp.zeros((16, 128), F32)
        for n in range(4):
            same = ids == (z * 4 + n).astype(F32)
            hits.append(jnp.sum(jnp.where(same, 1.0, 0.0), axis=0, keepdims=True))
            weights.append(jnp.sum(jnp.where(same, gates, 0.0), axis=0, keepdims=True))
            table = jnp.where(row == n, hits[n], table)
        places = jnp.dot(table.astype(BF16), tri[...], preferred_element_type=F32)
        slot = lax.broadcasted_iota(jnp.int32, (32, 128), 0).astype(F32)
        shift = jnp.where(first[0:1], 0.0, 16.0)
        chosen, weighted = [], []
        for n in range(4):
            mine = jnp.where(hits[n] > 0.5, places[n : n + 1] + shift, -1.0)
            chosen.append(jnp.where(slot == mine, 1.0, 0.0))
            weighted.append(chosen[n] * weights[n])
        chosen = jnp.concatenate(chosen, axis=0).astype(BF16)
        weighted = jnp.concatenate(weighted, axis=0)
        high = weighted.astype(BF16)
        pick[j, 0] = high
        pick[j, 1] = (weighted - high.astype(F32)).astype(BF16)
        for b in range(2):
            tokens = jnp.concatenate([ring_a[j + 1, b], ring_b[j, b]], axis=0)
            rows = jnp.dot(chosen, tokens, preferred_element_type=F32).astype(BF16)
            ybuf[j, :, :, pl.ds(b * 512, 512)] = rows.reshape(4, 32, 512)
        xfull[j, quarter, pl.ds(pl.multiple_of(y * 32, 32), 32), :] = ybuf[j, y]
        for r in range(1, 4):
            to_y(j, r).start()

    def stage_x1(j):
        for r in range(1, 4):
            to_y(j, r).wait_recv()
        for n in range(3):
            to_x(j, n).start()

    def stage_x2(j):
        for n in range(2):
            wait_x(j, n)
        to_x(j, 3).start()

    def wait_x(j, n):
        part = xfull.at[j, across, pl.ds(64 * n, 64), :]
        move(part, part, x_s.at[j, n], x_r.at[j, n], partner).wait_recv()

    def stage_m(j):
        for n in range(2, 4):
            to_x(j, n).wait_recv()
        total = jnp.zeros((128, 256), F32)
        for q in range(4):
            total += jnp.dot(xfull[j, q], wcat[q], preferred_element_type=F32)
        gate, lift = total[:, :128], total[:, 128:]
        hfull[j, tp] = (gate / (1.0 + jnp.exp(-gate)) * lift).astype(BF16)
        for n in range(4):
            to_h(j, n).start()

    def stage_h2(j):
        for n in range(3):
            to_h(j, n).wait_recv()
        for n in range(4, 7):
            to_h(j, n).start()

    def stage_d(j):
        for n in range(3, 7):
            to_h(j, n).wait_recv()
        units = jnp.concatenate([hfull[j, n] for n in range(8)], axis=1)
        rows = jnp.dot(units, wdv[...], preferred_element_type=F32).astype(BF16)
        obuf[j] = rows.reshape(4, 32, 512)
        oin[j, y] = obuf[j, y]
        for r in range(1, 4):
            to_o(j, r).start()

    def stage_c(j):
        for r in range(1, 4):
            to_o(j, r).wait_recv()
        rows = oin[j].reshape(128, 512)
        dims = (((0,), (0,)), ((), ()))
        total = lax.dot_general(pick[j, 0], rows, dims, preferred_element_type=F32)
        total += lax.dot_general(pick[j, 1], rows, dims, preferred_element_type=F32)
        cbuf[j, 0] = total[:64].astype(BF16)
        cbuf[j, 1] = total[64:].astype(BF16)

        for d in range(9):
            if d:
                @pl.when(j + 1 == d)
                def _():
                    if d in HOLDS:
                        own[1 + HOLDS.index(d), 0] = total[:64]
                    else:
                        home_a(d - 1, d).start()

            if d < 8:
                @pl.when(j == d)
                def _():
                    if d == 0:
                        own[0, 0] = total[64:]
                    elif d in HOLDS:
                        own[1 + HOLDS.index(d), 1] = total[64:]
                    else:
                        home_b(d, d).start()

        for b in range(PARTS + 1):
            up(j, b).wait_send()

            @pl.when(j < STEPS - 1)
            def _():
                down(j, b).wait_send()

        for r in range(1, 4):
            to_y(j, r).wait_send()
            to_o(j, r).wait_send()
        for n in range(4):
            to_x(j, n).wait_send()
        for n in range(7):
            to_h(j, n).wait_send()

    def stage(name, body, i):
        j = i - AT[name]

        @pl.when((j >= 0) & (j < STEPS))
        def _():
            body(j)

    @pl.loop(0, STEPS + AT["C"])
    def _(i):
        @pl.when(i <= STEPS)
        def _():
            for b in range(PARTS + 1):

                @pl.when(i > 0)
                def _():
                    up(i - 1, b).wait_recv()

                @pl.when(i < STEPS)
                def _():
                    up(i, b).start()

                @pl.when((i > 0) & (i < STEPS))
                def _():
                    down(i - 1, b).wait_recv()

                @pl.when(i < STEPS - 1)
                def _():
                    down(i, b).start()

        stage("Y", stage_y, i)
        stage("X1", stage_x1, i)
        stage("X2", stage_x2, i)
        stage("H2", stage_h2, i)
        stage("D", stage_d, i)
        stage("M", stage_m, i)
        stage("C", stage_c, i)

    for d in HOLDS:
        for n, home, zin in ((0, home_a, zin_a), (1, home_b, zin_b)):
            total = own[1 + HOLDS.index(d), n]
            for e in range(7 + (n == 0), d, -1):
                if NEXT[e] == d:
                    home(e - (n == 0), e).wait_recv()
                    total += zin[e - (n == 0)].astype(F32)
            cbuf[d - (n == 0), n] = total.astype(BF16)
            home(d - (n == 0), d).start()

    for r in range(1, 8):
        for b in range(3):
            spread(r, b).wait_send()
    total = own[0, 0] + hq[:, tp // 4].astype(F32).reshape(64, 512)
    for d in range(1, 9):
        if NEXT[d] == 0 and d not in HOLDS:
            home_a(d - 1, d).wait_recv()
            home_b(d, d).wait_recv()
            total += zin_a[d - 1].astype(F32) + zin_b[d].astype(F32)
    for d in range(1, 9):
        home_a(d - 1, d).wait_send()
        if d < 8:
            home_b(d, d).wait_send()
    for d in reversed(HOLDS):
        if NEXT[d] == 0:
            home_a(d - 1, d).wait_recv()
            home_b(d, d).wait_recv()
            total += zin_a[d - 1].astype(F32) + zin_b[d].astype(F32)
    out_ref[...] = total.astype(BF16)


def shards(hidden_in, norm_gain, expert_ids, gate_weights, w_gate, w_up, w_down):
    vmem, hbm = pl.BlockSpec(memory_space=pltpu.VMEM), pl.BlockSpec(memory_space=pl.ANY)
    dma = pltpu.SemaphoreType.DMA
    return pl.pallas_call(
        kernel,
        out_shape=jax.ShapeDtypeStruct((64, 512), BF16),
        in_specs=[vmem] * 4 + [hbm] * 3,
        out_specs=vmem,
        scratch_shapes=[
            pltpu.VMEM((8, 2, 8, 512), BF16),
            pltpu.VMEM((8, 8, 128), F32),
            pltpu.VMEM((9, 2, 64, 512), BF16),
            pltpu.VMEM((8, 2, 64, 512), BF16),
            pltpu.VMEM((9, 16, 128), F32),
            pltpu.VMEM((8, 16, 128), F32),
            pltpu.VMEM((8, 2, 128, 128), BF16),
            pltpu.VMEM((8, 4, 32, 1024), BF16),
            pltpu.VMEM((8, 4, 128, 1024), BF16),
            pltpu.VMEM((8, 8, 128, 128), BF16),
            pltpu.VMEM((8, 4, 32, 512), BF16),
            pltpu.VMEM((8, 4, 32, 512), BF16),
            pltpu.VMEM((8, 2, 64, 512), BF16),
            pltpu.VMEM((1 + len(HOLDS), 2, 64, 512), F32),
            pltpu.VMEM((8, 64, 512), BF16),
            pltpu.VMEM((8, 64, 512), BF16),
            pltpu.VMEM((4, 1024, 256), BF16),
            pltpu.VMEM((1024, 512), BF16),
            pltpu.VMEM((128, 128), BF16),
            dma((17,)),
            dma((7, 3)), dma((7, 3)),
            dma((8, PARTS + 1)), dma((8, PARTS + 1)),
            dma((7, PARTS + 1)), dma((7, PARTS + 1)),
            dma((8, 3)), dma((8, 3)),
            dma((8, 4)), dma((8, 4)),
            dma((8, 7)), dma((8, 7)),
            dma((8, 3)), dma((8, 3)),
            dma((8,)), dma((8,)),
            dma((8,)), dma((8,)),
        ],
        compiler_params=pltpu.CompilerParams(
            collective_id=0, has_side_effects=True, vmem_limit_bytes=56 * 1024 * 1024
        ),
    )(
        hidden_in,
        norm_gain,
        expert_ids.T,
        gate_weights.T,
        w_gate,
        w_up,
        w_down,
    )


def solution(mesh):
    in_specs = (
        P(("ep", "tp"), None),
        P(),
        P("ep", None),
        P("ep", None),
        P("ep", None, "tp"),
        P("ep", None, "tp"),
        P("ep", None, "tp"),
    )
    return jax.shard_map(shards, mesh=mesh, in_specs=in_specs, out_specs=P("ep", "tp"), check_vma=False)
```

```python
import functools

import jax
import jax.numpy as jnp
from jax import lax
from jax.experimental import pallas as pl
from jax.experimental.pallas import tpu as pltpu
from jax.sharding import PartitionSpec as P

MESH = pl.DeviceIdType.MESH
F32, BF16 = jnp.float32, jnp.bfloat16
CHUNKS = 16
PARTS = 2
AT = {'Y': 0, 'X1': 2, 'X2': 4, 'M': 6, 'H2': 8, 'D': 9, 'C': 12}


def kernel(
    hid_ref, gain_ref, ids_ref, gat_ref, wg_ref, wu_ref, wd_ref, out_ref,
    hq, scl, ring, meta, pick, ybuf, xfull, hfull, obuf, oin, cbuf, own, zin,
    wcat, wdv, tri,
    wsem, p_s, p_r, z_s, z_r, y_s, y_r, x_s, x_r, h_s, h_r, o_s, o_r, c_s, c_r,
):
    tp, ep = lax.axis_index("tp"), lax.axis_index("ep")
    x, c = tp // 2, lax.rem(tp, 2)
    z, y = ep // 4, lax.rem(ep, 4)
    quarter = lax.rem(tp, 4)
    across = lax.rem(quarter + 2, 4)

    def at_tp(r):
        return (lax.rem(tp + r + 8, 8), ep)

    def at_x(r):
        return (lax.rem(x + r + 4, 4) * 2 + c, ep)

    def at_y(r):
        return (tp, z * 4 + lax.rem(y + r, 4))

    def at_z(r):
        return (tp, lax.rem(z + r + 16, 16) * 4 + y)

    partner = (x * 2 + 1 - c, ep)

    def move(src, dst, send, recv, device):
        return pltpu.make_async_remote_copy(
            src_ref=src, dst_ref=dst, send_sem=send, recv_sem=recv, device_id=device, device_id_type=MESH
        )

    barrier = pltpu.get_barrier_semaphore()
    peers = [at_tp(r) for r in range(1, 8)] + [at_y(r) for r in range(1, 4)]
    peers += [at_z(r) for r in (-3, -2, -1, 1, 2, 3)]
    for peer in peers:
        pl.semaphore_signal(barrier, inc=1, device_id=peer, device_id_type=MESH)

    values = hid_ref[...].astype(F32)
    scale = lax.rsqrt(jnp.mean(values * values, axis=1, keepdims=True) + 1e-06)
    scl[tp] = jnp.broadcast_to(scale, (8, 128))
    for b in range(2):
        hq[tp, b] = hid_ref[:, pl.ds(pl.multiple_of((quarter + 4 * b) * 512, 512), 512)]
    pl.semaphore_wait(barrier, len(peers))

    def spread(r, b):
        device = at_tp(r)
        if b == 2:
            src, dst = scl.at[tp], scl.at[tp]
        else:
            block = lax.rem(device[0], 4) + 4 * b
            src, dst = hid_ref.at[:, pl.ds(pl.multiple_of(block * 512, 512), 512)], hq.at[tp, b]
        return move(src, dst, p_s.at[r - 1, b], p_r.at[r - 1, b], device)

    for r in range(1, 8):
        for b in range(3):
            spread(r, b).start()
    loads = []
    for q in range(4):
        for b in range(2):
            rows = pl.ds((q + 4 * b) * 512, 512)
            for n, w in enumerate((wg_ref, wu_ref)):
                loads.append(
                    pltpu.make_async_copy(
                        w.at[0, rows, :], wcat.at[q, pl.ds(b * 512, 512), pl.ds(n * 128, 128)], wsem.at[len(loads)]
                    )
                )
    loads.append(pltpu.make_async_copy(wd_ref.at[0], wdv, wsem.at[16]))
    for load in loads:
        load.start()
    ids, gates = ids_ref[...].astype(F32), gat_ref[...]
    table = jnp.concatenate(
        [jnp.concatenate([ids, ids], axis=1), jnp.concatenate([gates, gates], axis=1)], axis=0
    )
    meta[0] = table
    meta[1] = table
    before, after = lax.broadcasted_iota(jnp.int32, (64, 64), 0), lax.broadcasted_iota(jnp.int32, (64, 64), 1)
    tri[...] = (before < after).astype(F32).astype(BF16)
    for r in range(1, 8):
        for b in range(3):
            spread(r, b).wait_recv()
    scales = scl[...]
    scales = jnp.concatenate([scales] * 4, axis=2)
    for b in range(2):
        gain = gain_ref[pl.ds(pl.multiple_of((quarter + 4 * b) * 512, 512), 512)].astype(F32).reshape(1, 512)
        normed = (hq[:, b].astype(F32) * scales).reshape(64, 512) * gain
        normed = normed.astype(BF16)
        ring[0, b] = normed
        ring[1, b] = normed
    for load in loads:
        load.wait()

    def pass_on(r, b):
        if b == PARTS:
            src, dst = meta.at[r], meta.at[r + 2]
        else:
            cols = pl.ds(b * 1024 // PARTS % 512, 1024 // PARTS)
            src, dst = ring.at[r, b * 2 // PARTS, :, cols], ring.at[r + 2, b * 2 // PARTS, :, cols]
        return move(src, dst, z_s.at[r, b], z_r.at[r, b], at_z(1 - 2 * lax.rem(r, 2)))

    def to_y(j, r):
        device = at_y(r)
        there = lax.rem(y + r, 4)
        dst = xfull.at[j, quarter, pl.ds(pl.multiple_of(y * 16, 16), 16), :]
        return move(ybuf.at[j, there], dst, y_s.at[j, r - 1], y_r.at[j, r - 1], device)

    def to_x(j, n):
        if n == 0:
            part, device = xfull.at[j, quarter, pl.ds(0, 32), :], at_x(1)
        elif n == 1:
            part, device = xfull.at[j, quarter, pl.ds(32, 32), :], at_x(-1)
        elif n == 2:
            part, device = xfull.at[j, quarter], partner
        else:
            part, device = xfull.at[j, across], partner
        return move(part, part, x_s.at[j, n], x_r.at[j, n], device)

    def to_h(j, n):
        if n < 3:
            part, device = hfull.at[j, tp], at_x(n + 1)
        elif n == 3:
            part, device = hfull.at[j, tp], partner
        else:
            part, device = hfull.at[j, lax.rem(tp - 2 * (n - 3) + 8, 8)], partner
        return move(part, part, h_s.at[j, n], h_r.at[j, n], device)

    def to_o(j, r):
        return move(obuf.at[j, lax.rem(y + r, 4)], oin.at[j, y], o_s.at[j, r - 1], o_r.at[j, r - 1], at_y(r))

    def home(j, hops):
        away = (2 * lax.rem(j + 1, 2) - 1) * hops
        return move(cbuf.at[j], zin.at[j], c_s.at[j], c_r.at[j], at_z(away))

    def stage_y(j):
        ids, gates = meta[j + 1, 0:8, 0:64], meta[j + 1, 8:16, 0:64]
        row = lax.broadcasted_iota(jnp.int32, (16, 64), 0)
        hits, weights, table = [], [], jnp.zeros((16, 64), F32)
        for n in range(4):
            same = ids == (z * 4 + n).astype(F32)
            hits.append(jnp.sum(jnp.where(same, 1.0, 0.0), axis=0, keepdims=True))
            weights.append(jnp.sum(jnp.where(same, gates, 0.0), axis=0, keepdims=True))
            table = jnp.where(row == n, hits[n], table)
        places = jnp.dot(table.astype(BF16), tri[...], preferred_element_type=F32)
        slot = row.astype(F32)
        chosen, weighted = [], []
        for n in range(4):
            mine = jnp.where(hits[n] > 0.5, places[n : n + 1], -1.0)
            chosen.append(jnp.where(slot == mine, 1.0, 0.0))
            weighted.append(chosen[n] * weights[n])
        chosen = jnp.concatenate(chosen, axis=0).astype(BF16)
        weighted = jnp.concatenate(weighted, axis=0)
        high = weighted.astype(BF16)
        pick[j, 0] = high
        pick[j, 1] = (weighted - high.astype(F32)).astype(BF16)
        for b in range(2):
            rows = jnp.dot(chosen, ring[j + 1, b], preferred_element_type=F32).astype(BF16)
            ybuf[j, :, :, pl.ds(b * 512, 512)] = rows.reshape(4, 16, 512)
        xfull[j, quarter, pl.ds(pl.multiple_of(y * 16, 16), 16), :] = ybuf[j, y]
        for r in range(1, 4):
            to_y(j, r).start()

    def stage_x1(j):
        for r in range(1, 4):
            to_y(j, r).wait_recv()
        for n in range(3):
            to_x(j, n).start()

    def stage_x2(j):
        for n in range(2):
            wait_x(j, n)
        to_x(j, 3).start()

    def wait_x(j, n):
        part = xfull.at[j, across, pl.ds(32 * n, 32), :]
        move(part, part, x_s.at[j, n], x_r.at[j, n], partner).wait_recv()

    def stage_m(j):
        for n in range(2, 4):
            to_x(j, n).wait_recv()
        total = jnp.zeros((64, 256), F32)
        for q in range(4):
            total += jnp.dot(xfull[j, q], wcat[q], preferred_element_type=F32)
        gate, lift = total[:, :128], total[:, 128:]
        hfull[j, tp] = (gate / (1.0 + jnp.exp(-gate)) * lift).astype(BF16)
        for n in range(4):
            to_h(j, n).start()

    def stage_h2(j):
        for n in range(3):
            to_h(j, n).wait_recv()
        for n in range(4, 7):
            to_h(j, n).start()

    def stage_d(j):
        for n in range(3, 7):
            to_h(j, n).wait_recv()
        units = jnp.concatenate([hfull[j, n] for n in range(8)], axis=1)
        rows = jnp.dot(units, wdv[...], preferred_element_type=F32).astype(BF16)
        obuf[j] = rows.reshape(4, 16, 512)
        oin[j, y] = obuf[j, y]
        for r in range(1, 4):
            to_o(j, r).start()

    def stage_c(j):
        for r in range(1, 4):
            to_o(j, r).wait_recv()
        rows = oin[j].reshape(64, 512)
        dims = (((0,), (0,)), ((), ()))
        total = lax.dot_general(pick[j, 0], rows, dims, preferred_element_type=F32)
        total += lax.dot_general(pick[j, 1], rows, dims, preferred_element_type=F32)
        cbuf[j] = total.astype(BF16)
        distance = (j + 1) // 2

        @pl.when(lax.rem(distance, 3) > 0)
        def _():
            home(j, lax.rem(distance, 3)).start()

        @pl.when(lax.rem(distance, 3) == 0)
        def _():
            own[distance // 3, lax.rem(j, 2)] = total

        @pl.when(j < 15)
        def _():
            for b in range(PARTS + 1):
                pass_on(j, b).wait_send()

        for r in range(1, 4):
            to_y(j, r).wait_send()
            to_o(j, r).wait_send()
        for n in range(4):
            to_x(j, n).wait_send()
        for n in range(7):
            to_h(j, n).wait_send()

    def stage(name, body, i):
        j = i - AT[name]

        @pl.when((j >= 0) & (j < CHUNKS))
        def _():
            body(j)

    for r in range(2):
        for b in range(PARTS + 1):
            pass_on(r, b).start()

    @pl.loop(0, CHUNKS + AT["C"])
    def _(i):
        @pl.when((i > 0) & (i < CHUNKS))
        def _():
            for b in range(PARTS + 1):
                pass_on(i - 1, b).wait_recv()

                @pl.when(i < 14)
                def _():
                    pass_on(i + 1, b).start()

        stage("Y", stage_y, i)
        stage("C", stage_c, i)
        stage("X1", stage_x1, i)
        stage("M", stage_m, i)
        stage("D", stage_d, i)
        stage("X2", stage_x2, i)
        stage("H2", stage_h2, i)

    for d in (6, 3):
        for j in (2 * d - 1, 2 * d):
            total = own[d // 3, j % 2]
            for e in range(j + 6 if d == 3 else j + 4, j, -2):
                if e < CHUNKS:
                    home(e, 0).wait_recv()
                    total += zin[e].astype(F32)
            cbuf[j] = total.astype(BF16)
            home(j, 3).start()

    for r in range(1, 8):
        for b in range(3):
            spread(r, b).wait_send()
    total = own[0, 0] + hq[:, tp // 4].astype(F32).reshape(64, 512)
    for j in range(1, 5):
        home(j, 0).wait_recv()
        total += zin[j].astype(F32)
    for j in range(1, CHUNKS):
        home(j, 0).wait_send()
    for j in range(5, 7):
        home(j, 0).wait_recv()
        total += zin[j].astype(F32)
    out_ref[...] = total.astype(BF16)


def shards(hidden_in, norm_gain, expert_ids, gate_weights, w_gate, w_up, w_down):
    vmem, hbm = pl.BlockSpec(memory_space=pltpu.VMEM), pl.BlockSpec(memory_space=pl.ANY)
    dma = pltpu.SemaphoreType.DMA
    return pl.pallas_call(
        kernel,
        out_shape=jax.ShapeDtypeStruct((64, 512), BF16),
        in_specs=[vmem] * 4 + [hbm] * 3,
        out_specs=vmem,
        scratch_shapes=[
            pltpu.VMEM((8, 2, 8, 512), BF16),
            pltpu.VMEM((8, 8, 128), F32),
            pltpu.VMEM((17, 2, 64, 512), BF16),
            pltpu.VMEM((17, 16, 128), F32),
            pltpu.VMEM((16, 2, 64, 64), BF16),
            pltpu.VMEM((16, 4, 16, 1024), BF16),
            pltpu.VMEM((16, 4, 64, 1024), BF16),
            pltpu.VMEM((16, 8, 64, 128), BF16),
            pltpu.VMEM((16, 4, 16, 512), BF16),
            pltpu.VMEM((16, 4, 16, 512), BF16),
            pltpu.VMEM((16, 64, 512), BF16),
            pltpu.VMEM((3, 2, 64, 512), F32),
            pltpu.VMEM((16, 64, 512), BF16),
            pltpu.VMEM((4, 1024, 256), BF16),
            pltpu.VMEM((1024, 512), BF16),
            pltpu.VMEM((64, 64), BF16),
            dma((17,)),
            dma((7, 3)), dma((7, 3)),
            dma((15, PARTS + 1)), dma((15, PARTS + 1)),
            dma((16, 3)), dma((16, 3)),
            dma((16, 4)), dma((16, 4)),
            dma((16, 7)), dma((16, 7)),
            dma((16, 3)), dma((16, 3)),
            dma((16,)), dma((16,)),
        ],
        compiler_params=pltpu.CompilerParams(
            collective_id=0, has_side_effects=True, vmem_limit_bytes=56 * 1024 * 1024
        ),
    )(
        hidden_in,
        norm_gain,
        expert_ids.T,
        gate_weights.T,
        w_gate,
        w_up,
        w_down,
    )


def solution(mesh):
    in_specs = (
        P(("ep", "tp"), None),
        P(),
        P("ep", None),
        P("ep", None),
        P("ep", None, "tp"),
        P("ep", None, "tp"),
        P("ep", None, "tp"),
    )
    return jax.shard_map(shards, mesh=mesh, in_specs=in_specs, out_specs=P("ep", "tp"), check_vma=False)
```

```python
import functools

import jax
import jax.numpy as jnp
from jax import lax
from jax.experimental import pallas as pl
from jax.experimental.pallas import tpu as pltpu
from jax.sharding import PartitionSpec as P

MESH = pl.DeviceIdType.MESH
F32, BF16 = jnp.float32, jnp.bfloat16
CHUNKS = 16
PARTS = 2
AT = {'Y': 0, 'X1': 2, 'X2': 4, 'M': 6, 'H2': 8, 'D': 9, 'C': 12}


def kernel(
    hid_in, gain_in, ids_in, gat_in, wg_ref, wu_ref, wd_ref, out_ref,
    hid_ref, gain_ref, ids_ref, gat_ref,
    hq, scl, ring, meta, pick, ybuf, xfull, hfull, obuf, oin, cbuf, own, zin,
    wcat, wdv, tri,
    isem, wsem, p_s, p_r, z_s, z_r, y_s, y_r, x_s, x_r, h_s, h_r, o_s, o_r, c_s, c_r,
):
    tp, ep = lax.axis_index("tp"), lax.axis_index("ep")
    x, c = tp // 2, lax.rem(tp, 2)
    z, y = ep // 4, lax.rem(ep, 4)
    quarter = lax.rem(tp, 4)
    across = lax.rem(quarter + 2, 4)

    def at_tp(r):
        return (lax.rem(tp + r + 8, 8), ep)

    def at_x(r):
        return (lax.rem(x + r + 4, 4) * 2 + c, ep)

    def at_y(r):
        return (tp, z * 4 + lax.rem(y + r, 4))

    def at_z(r):
        return (tp, lax.rem(z + r + 16, 16) * 4 + y)

    partner = (x * 2 + 1 - c, ep)

    def move(src, dst, send, recv, device):
        return pltpu.make_async_remote_copy(
            src_ref=src, dst_ref=dst, send_sem=send, recv_sem=recv, device_id=device, device_id_type=MESH
        )

    barrier = pltpu.get_barrier_semaphore()
    peers = [at_tp(r) for r in range(1, 8)] + [at_y(r) for r in range(1, 4)]
    peers += [at_z(r) for r in (-3, -2, -1, 1, 2, 3)]
    for peer in peers:
        pl.semaphore_signal(barrier, inc=1, device_id=peer, device_id_type=MESH)

    takes = [
        pltpu.make_async_copy(src, dst, isem.at[n])
        for n, (src, dst) in enumerate(
            ((hid_in, hid_ref), (gain_in, gain_ref), (ids_in, ids_ref), (gat_in, gat_ref))
        )
    ]
    for take in takes:
        take.start()
    for take in takes:
        take.wait()
    values = hid_ref[...].astype(F32)
    scale = lax.rsqrt(jnp.mean(values * values, axis=1, keepdims=True) + 1e-06)
    scl[tp] = jnp.broadcast_to(scale, (8, 128))
    for b in range(2):
        hq[tp, b] = hid_ref[:, pl.ds(pl.multiple_of((quarter + 4 * b) * 512, 512), 512)]
    pl.semaphore_wait(barrier, len(peers))

    def spread(r, b):
        device = at_tp(r)
        if b == 2:
            src, dst = scl.at[tp], scl.at[tp]
        else:
            block = lax.rem(device[0], 4) + 4 * b
            src, dst = hid_ref.at[:, pl.ds(pl.multiple_of(block * 512, 512), 512)], hq.at[tp, b]
        return move(src, dst, p_s.at[r - 1, b], p_r.at[r - 1, b], device)

    for r in range(1, 8):
        for b in range(3):
            spread(r, b).start()
    loads = []
    for q in range(4):
        for b in range(2):
            rows = pl.ds((q + 4 * b) * 512, 512)
            for n, w in enumerate((wg_ref, wu_ref)):
                loads.append(
                    pltpu.make_async_copy(
                        w.at[0, rows, :], wcat.at[q, pl.ds(b * 512, 512), pl.ds(n * 128, 128)], wsem.at[len(loads)]
                    )
                )
    loads.append(pltpu.make_async_copy(wd_ref.at[0], wdv, wsem.at[16]))
    for load in loads:
        load.start()
    ids, gates = ids_ref[...].astype(F32), gat_ref[...]
    table = jnp.concatenate(
        [jnp.concatenate([ids, ids], axis=1), jnp.concatenate([gates, gates], axis=1)], axis=0
    )
    meta[0] = table
    meta[1] = table
    before, after = lax.broadcasted_iota(jnp.int32, (64, 64), 0), lax.broadcasted_iota(jnp.int32, (64, 64), 1)
    tri[...] = (before < after).astype(F32).astype(BF16)
    for r in range(1, 8):
        for b in range(3):
            spread(r, b).wait_recv()
    scales = scl[...]
    scales = jnp.concatenate([scales] * 4, axis=2)
    for b in range(2):
        gain = gain_ref[pl.ds(pl.multiple_of((quarter + 4 * b) * 512, 512), 512)].astype(F32).reshape(1, 512)
        normed = (hq[:, b].astype(F32) * scales).reshape(64, 512) * gain
        normed = normed.astype(BF16)
        ring[0, b] = normed
        ring[1, b] = normed
    for load in loads:
        load.wait()

    def pass_on(r, b):
        if b == PARTS:
            src, dst = meta.at[r], meta.at[r + 2]
        else:
            cols = pl.ds(b * 1024 // PARTS % 512, 1024 // PARTS)
            src, dst = ring.at[r, b * 2 // PARTS, :, cols], ring.at[r + 2, b * 2 // PARTS, :, cols]
        return move(src, dst, z_s.at[r, b], z_r.at[r, b], at_z(1 - 2 * lax.rem(r, 2)))

    def to_y(j, r):
        device = at_y(r)
        there = lax.rem(y + r, 4)
        dst = xfull.at[j, quarter, pl.ds(pl.multiple_of(y * 16, 16), 16), :]
        return move(ybuf.at[j, there], dst, y_s.at[j, r - 1], y_r.at[j, r - 1], device)

    def to_x(j, n):
        if n == 0:
            part, device = xfull.at[j, quarter, pl.ds(0, 32), :], at_x(1)
        elif n == 1:
            part, device = xfull.at[j, quarter, pl.ds(32, 32), :], at_x(-1)
        elif n == 2:
            part, device = xfull.at[j, quarter], partner
        else:
            part, device = xfull.at[j, across], partner
        return move(part, part, x_s.at[j, n], x_r.at[j, n], device)

    def to_h(j, n):
        if n < 3:
            part, device = hfull.at[j, tp], at_x(n + 1)
        elif n == 3:
            part, device = hfull.at[j, tp], partner
        else:
            part, device = hfull.at[j, lax.rem(tp - 2 * (n - 3) + 8, 8)], partner
        return move(part, part, h_s.at[j, n], h_r.at[j, n], device)

    def to_o(j, r):
        return move(obuf.at[j, lax.rem(y + r, 4)], oin.at[j, y], o_s.at[j, r - 1], o_r.at[j, r - 1], at_y(r))

    def home(j, hops):
        away = (2 * lax.rem(j + 1, 2) - 1) * hops
        return move(cbuf.at[j], zin.at[j], c_s.at[j], c_r.at[j], at_z(away))

    def stage_y(j):
        ids, gates = meta[j + 1, 0:8, 0:64], meta[j + 1, 8:16, 0:64]
        row = lax.broadcasted_iota(jnp.int32, (16, 64), 0)
        hits, weights, table = [], [], jnp.zeros((16, 64), F32)
        for n in range(4):
            same = ids == (z * 4 + n).astype(F32)
            hits.append(jnp.sum(jnp.where(same, 1.0, 0.0), axis=0, keepdims=True))
            weights.append(jnp.sum(jnp.where(same, gates, 0.0), axis=0, keepdims=True))
            table = jnp.where(row == n, hits[n], table)
        places = jnp.dot(table.astype(BF16), tri[...], preferred_element_type=F32)
        slot = row.astype(F32)
        chosen, weighted = [], []
        for n in range(4):
            mine = jnp.where(hits[n] > 0.5, places[n : n + 1], -1.0)
            chosen.append(jnp.where(slot == mine, 1.0, 0.0))
            weighted.append(chosen[n] * weights[n])
        chosen = jnp.concatenate(chosen, axis=0).astype(BF16)
        weighted = jnp.concatenate(weighted, axis=0)
        high = weighted.astype(BF16)
        pick[j, 0] = high
        pick[j, 1] = (weighted - high.astype(F32)).astype(BF16)
        for b in range(2):
            rows = jnp.dot(chosen, ring[j + 1, b], preferred_element_type=F32).astype(BF16)
            ybuf[j, :, :, pl.ds(b * 512, 512)] = rows.reshape(4, 16, 512)
        xfull[j, quarter, pl.ds(pl.multiple_of(y * 16, 16), 16), :] = ybuf[j, y]
        for r in range(1, 4):
            to_y(j, r).start()

    def stage_x1(j):
        for r in range(1, 4):
            to_y(j, r).wait_recv()
        for n in range(3):
            to_x(j, n).start()

    def stage_x2(j):
        for n in range(2):
            wait_x(j, n)
        to_x(j, 3).start()

    def wait_x(j, n):
        part = xfull.at[j, across, pl.ds(32 * n, 32), :]
        move(part, part, x_s.at[j, n], x_r.at[j, n], partner).wait_recv()

    def stage_m(j):
        for n in range(2, 4):
            to_x(j, n).wait_recv()
        total = jnp.zeros((64, 256), F32)
        for q in range(4):
            total += jnp.dot(xfull[j, q], wcat[q], preferred_element_type=F32)
        gate, lift = total[:, :128], total[:, 128:]
        hfull[j, tp] = (gate / (1.0 + jnp.exp(-gate)) * lift).astype(BF16)
        for n in range(4):
            to_h(j, n).start()

    def stage_h2(j):
        for n in range(3):
            to_h(j, n).wait_recv()
        for n in range(4, 7):
            to_h(j, n).start()

    def stage_d(j):
        for n in range(3, 7):
            to_h(j, n).wait_recv()
        units = jnp.concatenate([hfull[j, n] for n in range(8)], axis=1)
        rows = jnp.dot(units, wdv[...], preferred_element_type=F32).astype(BF16)
        obuf[j] = rows.reshape(4, 16, 512)
        oin[j, y] = obuf[j, y]
        for r in range(1, 4):
            to_o(j, r).start()

    def stage_c(j):
        for r in range(1, 4):
            to_o(j, r).wait_recv()
        rows = oin[j].reshape(64, 512)
        dims = (((0,), (0,)), ((), ()))
        total = lax.dot_general(pick[j, 0], rows, dims, preferred_element_type=F32)
        total += lax.dot_general(pick[j, 1], rows, dims, preferred_element_type=F32)
        cbuf[j] = total.astype(BF16)
        distance = (j + 1) // 2

        @pl.when(lax.rem(distance, 3) > 0)
        def _():
            home(j, lax.rem(distance, 3)).start()

        @pl.when(lax.rem(distance, 3) == 0)
        def _():
            own[distance // 3, lax.rem(j, 2)] = total

        @pl.when(j < 15)
        def _():
            for b in range(PARTS + 1):
                pass_on(j, b).wait_send()

        for r in range(1, 4):
            to_y(j, r).wait_send()
            to_o(j, r).wait_send()
        for n in range(4):
            to_x(j, n).wait_send()
        for n in range(7):
            to_h(j, n).wait_send()

    def stage(name, body, i):
        j = i - AT[name]

        @pl.when((j >= 0) & (j < CHUNKS))
        def _():
            body(j)

    for r in range(2):
        for b in range(PARTS + 1):
            pass_on(r, b).start()

    @pl.loop(0, CHUNKS + AT["C"])
    def _(i):
        @pl.when((i > 0) & (i < CHUNKS))
        def _():
            for b in range(PARTS + 1):
                pass_on(i - 1, b).wait_recv()

                @pl.when(i < 14)
                def _():
                    pass_on(i + 1, b).start()

        stage("Y", stage_y, i)
        stage("C", stage_c, i)
        stage("X1", stage_x1, i)
        stage("M", stage_m, i)
        stage("D", stage_d, i)
        stage("X2", stage_x2, i)
        stage("H2", stage_h2, i)

    for d in (6, 3):
        for j in (2 * d - 1, 2 * d):
            total = own[d // 3, j % 2]
            for e in range(j + 6 if d == 3 else j + 4, j, -2):
                if e < CHUNKS:
                    home(e, 0).wait_recv()
                    total += zin[e].astype(F32)
            cbuf[j] = total.astype(BF16)
            home(j, 3).start()

    for r in range(1, 8):
        for b in range(3):
            spread(r, b).wait_send()
    total = own[0, 0] + hq[:, tp // 4].astype(F32).reshape(64, 512)
    for j in range(1, 5):
        home(j, 0).wait_recv()
        total += zin[j].astype(F32)
    for j in range(1, CHUNKS):
        home(j, 0).wait_send()
    for j in range(5, 7):
        home(j, 0).wait_recv()
        total += zin[j].astype(F32)
    out_ref[...] = total.astype(BF16)


def shards(hidden_in, norm_gain, expert_ids, gate_weights, w_gate, w_up, w_down):
    vmem, hbm = pl.BlockSpec(memory_space=pltpu.VMEM), pl.BlockSpec(memory_space=pl.ANY)
    dma = pltpu.SemaphoreType.DMA
    return pl.pallas_call(
        kernel,
        out_shape=jax.ShapeDtypeStruct((64, 512), BF16),
        in_specs=[hbm] * 7,
        out_specs=vmem,
        scratch_shapes=[
            pltpu.VMEM((8, 4096), BF16),
            pltpu.VMEM((4096,), BF16),
            pltpu.VMEM((8, 64), jnp.int32),
            pltpu.VMEM((8, 64), F32),
            pltpu.VMEM((8, 2, 8, 512), BF16),
            pltpu.VMEM((8, 8, 128), F32),
            pltpu.VMEM((17, 2, 64, 512), BF16),
            pltpu.VMEM((17, 16, 128), F32),
            pltpu.VMEM((16, 2, 64, 64), BF16),
            pltpu.VMEM((16, 4, 16, 1024), BF16),
            pltpu.VMEM((16, 4, 64, 1024), BF16),
            pltpu.VMEM((16, 8, 64, 128), BF16),
            pltpu.VMEM((16, 4, 16, 512), BF16),
            pltpu.VMEM((16, 4, 16, 512), BF16),
            pltpu.VMEM((16, 64, 512), BF16),
            pltpu.VMEM((3, 2, 64, 512), F32),
            pltpu.VMEM((16, 64, 512), BF16),
            pltpu.VMEM((4, 1024, 256), BF16),
            pltpu.VMEM((1024, 512), BF16),
            pltpu.VMEM((64, 64), BF16),
            dma((4,)),
            dma((17,)),
            dma((7, 3)), dma((7, 3)),
            dma((15, PARTS + 1)), dma((15, PARTS + 1)),
            dma((16, 3)), dma((16, 3)),
            dma((16, 4)), dma((16, 4)),
            dma((16, 7)), dma((16, 7)),
            dma((16, 3)), dma((16, 3)),
            dma((16,)), dma((16,)),
        ],
        compiler_params=pltpu.CompilerParams(
            collective_id=0, has_side_effects=True, vmem_limit_bytes=56 * 1024 * 1024
        ),
    )(
        hidden_in,
        norm_gain,
        expert_ids.T,
        gate_weights.T,
        w_gate,
        w_up,
        w_down,
    )


def solution(mesh):
    in_specs = (
        P(("ep", "tp"), None),
        P(),
        P("ep", None),
        P("ep", None),
        P("ep", None, "tp"),
        P("ep", None, "tp"),
        P("ep", None, "tp"),
    )
    return jax.shard_map(shards, mesh=mesh, in_specs=in_specs, out_specs=P("ep", "tp"), check_vma=False)
```
